128 devices in a mesh: ia: 4 (over x_lo, core), ja: 16 (over y, z), ka: 2 (over x_hi).
Axes of the slice: x: 4 (x_hi: 2, x_lo: 2; x = x_hi * 2 + x_lo), y: 4, z: 4, core: 2. Of those that a mesh axis runs over, the one named last changes fastest.
Arguments:
- tensor: bfloat16 [768, 1024, 256], P('ia', 'ja', 'ka'), may hold values from -190 to 190
- matrix: bfloat16 [768, 16384], P('ia', ('ja', 'ka')), may hold values from -160 to 160
- second_in: float32 [1024, 256], P('ja'), may hold values from -10 to 10
- third_in: float32 [256, 256], P('ka'), may hold values from -10 to 10
- column_in: float32 [16384, 256], P(('ja', 'ka')), may hold values from -510 to 510
Outputs:
- first_out: float32 [768, 256], P(('ia', 'ja', 'ka'))
- second_out: float32 [16, 64, 256], P('ja', ('ia', 'ka'))
- third_out: float32 [2, 128, 256], P('ka', ('ia', 'ja'))
- column_out: float32 [32, 512, 256], P(('ja', 'ka'), 'ia')
The draws below stay inside these ranges and needn't reach their ends.
All inputs are finite; a program needn't handle non-finite values.
Results may differ from the reference program's by a relative error of at most 0.02.
Values may be sent and summed in bfloat16 or wider, within the bound.
No kernel may reach another device: no remote copies, remote signals or barrier semaphores. Data moves between devices by JAX's collectives and lax.ppermute only.
A program may use at most 64 MiB of HBM per device.

```python
import math
import jax
import jax.numpy as jnp
from jax import lax

R = 256
JB = 64
KB = 128
MB = 512
I = 768
J = 1024
K = 256
M = 16384


def ramp(length, end_ratio):
    position = jnp.arange(length, dtype=jnp.float32) / max(length - 1, 1)
    return jnp.exp(math.log(end_ratio) * (position - 0.5))


def draw_tensor(key, part):
    subkeys = jax.random.split(jax.random.fold_in(key, 11), 1)
    noise_cells = jnp.clip(jax.random.normal(subkeys[0], (I, J, K), jnp.float32), -4.0, 4.0)
    profile = ramp(I, math.sqrt(10.0))[:, None, None] * ramp(J, math.sqrt(10.0))[None, :, None] * ramp(K, math.sqrt(10.0))[None, None, :]
    values = profile * noise_cells
    return values.astype(jnp.bfloat16)


def draw_matrix(key, part):
    subkeys = jax.random.split(jax.random.fold_in(key, 23), 1)
    noise_cells = jnp.clip(jax.random.normal(subkeys[0], (I, M), jnp.float32), -4.0, 4.0)
    profile = ramp(I, math.sqrt(10.0))[:, None] * ramp(M, math.sqrt(10.0))[None, :]
    values = 3.0 * profile * noise_cells
    return values.astype(jnp.bfloat16)


def factor_draw(key, length):
    subkeys = jax.random.split(key, 3)
    row_common = jnp.clip(jax.random.normal(subkeys[1], (length,), jnp.float32), -3.0, 3.0)
    column_weight = 1.0 + 0.5 * jnp.clip(jax.random.normal(subkeys[2], (R,), jnp.float32), -3.0, 3.0)
    noise_cells = jnp.clip(jax.random.normal(subkeys[0], (length, R), jnp.float32), -4.0, 4.0)
    return noise_cells + 0.7 * row_common[:, None] * column_weight[None, :]


def draw_second_in(key, part):
    return factor_draw(jax.random.fold_in(key, 31), J)


def draw_third_in(key, part):
    return factor_draw(jax.random.fold_in(key, 37), K)


def draw_column_in(key, part):
    base = factor_draw(jax.random.fold_in(key, 41), M)
    weight_scale = math.sqrt(J * K / M)
    profile = ramp(M, 4.0)
    return base * profile[:, None] * weight_scale


def setup_inputs(seed: int = 0) -> dict:
    streams_of = jax.random.split(jax.random.key(seed), 6)
    return {
        "tensor": draw_tensor(jax.random.fold_in(streams_of[5], 71), 0),
        "matrix": draw_matrix(jax.random.fold_in(streams_of[5], 71), 0),
        "second_in": draw_second_in(jax.random.fold_in(streams_of[5], 71), 0),
        "third_in": draw_third_in(jax.random.fold_in(streams_of[5], 71), 0),
        "column_in": draw_column_in(jax.random.fold_in(streams_of[5], 71), 0),
    }


def gram_of(factor):
    return jnp.dot(factor.T.astype(jnp.float32), factor.astype(jnp.float32), precision=lax.Precision.HIGHEST, preferred_element_type=jnp.float32)

def solve_rows(right_side, system):
    lower_factor = jnp.linalg.cholesky(system)
    return jax.scipy.linalg.cho_solve((lower_factor, True), right_side.T).T

def normalize(unscaled):
    return unscaled * lax.rsqrt(lax.optimization_barrier(jnp.mean(unscaled * unscaled, axis=0)) + 1e-06)

def reference(tensor, matrix, second_in, third_in, column_in):
    gram_second = gram_of(second_in)
    gram_third = gram_of(third_in)
    gram_column = gram_of(column_in)
    column_half = column_in.astype(jnp.bfloat16)
    weights_one = (second_in[:, None, :] * third_in[None, :, :]).astype(jnp.bfloat16)
    partial_one = lax.dot_general(tensor.astype(jnp.float32), weights_one.astype(jnp.float32), (((1, 2), (0, 1)), ((), ())), preferred_element_type=jnp.float32)
    partial_one = partial_one + jnp.dot(matrix.astype(jnp.float32), column_half.astype(jnp.float32), preferred_element_type=jnp.float32)
    first_new = normalize(solve_rows(partial_one, gram_second * gram_third + gram_column))
    gram_first = gram_of(first_new)
    first_half = first_new.astype(jnp.bfloat16)
    weights_two = (first_half.astype(jnp.float32)[:, None, :] * third_in[None, :, :]).astype(jnp.bfloat16)
    partial_two = lax.dot_general(tensor.astype(jnp.float32), weights_two.astype(jnp.float32), (((0, 2), (0, 1)), ((), ())), preferred_element_type=jnp.float32)
    second_new = normalize(solve_rows(partial_two, gram_first * gram_third))
    gram_updated = gram_of(second_new)
    second_half = second_new.astype(jnp.bfloat16)
    tensor_blocks = tensor.reshape(I // 32, 32, J, K)
    half_blocks = first_half.reshape(I // 32, 32, R)

    def add_block(running, slab_pair):
        tensor_slab, half_slab = slab_pair
        weights_three = half_slab[:, None, :] * second_half[None, :, :]
        term = lax.dot_general(tensor_slab.astype(jnp.float32), weights_three.astype(jnp.float32), (((0, 1), (0, 1)), ((), ())), preferred_element_type=jnp.float32)
        return (running + term, None)
    partial_three, unused = lax.scan(add_block, jnp.zeros((K, R), jnp.float32), (tensor_blocks, half_blocks))
    third_new = normalize(solve_rows(partial_three, gram_first * gram_updated))
    partial_column = lax.dot_general(matrix.astype(jnp.float32), first_half.astype(jnp.float32), (((0,), (0,)), ((), ())), preferred_element_type=jnp.float32)
    column_new = normalize(solve_rows(partial_column, gram_first))
    return (first_new, second_new.reshape(J // JB, JB, R), third_new.reshape(K // KB, KB, R), column_new.reshape(M // MB, MB, R))
```

```python
import jax
import jax.numpy as jnp
from jax import lax
from jax.sharding import PartitionSpec as P

ALL = ("ia", "ja", "ka")
HI = lax.Precision.HIGHEST


def gram_of(factor):
    return lax.dot_general(
        factor, factor, (((0,), (0,)), ((), ())), precision=HI, preferred_element_type=jnp.float32
    )


def matmul(left, right):
    return jnp.dot(left, right, precision=HI, preferred_element_type=jnp.float32)


def inverse_factor(system):
    lower = jnp.linalg.cholesky(system)
    eye = jnp.eye(system.shape[0], dtype=jnp.float32)
    return lax.linalg.triangular_solve(lower, eye, left_side=True, lower=True)


def solve_rows(right_side, factor):
    return matmul(matmul(right_side, factor.T), factor)


def exchange(blocks, axes):
    return lax.all_to_all(blocks, axes, 0, 0, tiled=True)


def reduce_rows(whole, axes, parts):
    rows, width = whole.shape
    return jnp.sum(exchange(whole.reshape(parts, rows // parts, width), axes), axis=0)


def gather_rows(rows, axes, parts):
    return exchange(jnp.broadcast_to(rows[None], (parts,) + rows.shape), axes)


def column_scale(unscaled, row_total):
    return lax.rsqrt(jnp.sum(unscaled * unscaled, axis=0) / row_total + 1e-06)


def body(tensor, matrix, second_in, third_in, column_in):
    span_first, span_second, span_third = tensor.shape
    span_column = matrix.shape[1]
    rank = second_in.shape[1]
    n_ia, n_ja, n_ka = (lax.axis_size(a) for a in ALL)
    n_all = n_ia * n_ja * n_ka
    n_jk = n_ja * n_ka
    at_ia, at_ja, at_ka = (lax.axis_index(a) for a in ALL)
    at = (at_ia * n_ja + at_ja) * n_ka + at_ka

    part_second = span_second // n_ka
    part_third = span_third // n_ja
    slab = rank // n_ia
    grams = [
        gram_of(lax.dynamic_slice_in_dim(second_in, at_ka * part_second, part_second, 0)),
        gram_of(lax.dynamic_slice_in_dim(third_in, at_ja * part_third, part_third, 0)),
        gram_of(column_in),
    ]
    slabs = [
        lax.dynamic_slice_in_dim(g, at_ia * slab, slab, 0).reshape(n_jk, slab // n_jk, rank)
        for g in grams
    ]
    per = slab // n_jk
    sums = jnp.sum(exchange(jnp.concatenate(slabs, axis=1), ("ja", "ka")), axis=0)
    gs, gt, gc = sums[:per], sums[per : 2 * per], sums[2 * per :]
    gathered = gather_rows(jnp.concatenate([gs * gt + gc, gt], axis=0), ALL, n_all)
    system_one = gathered[:, :per].reshape(rank, rank)
    gram_third = gathered[:, per:].reshape(rank, rank)

    column_half = column_in.astype(jnp.bfloat16)
    weights_one = (second_in[:, None, :] * third_in[None, :, :]).astype(jnp.bfloat16)
    weights_one = lax.optimization_barrier(weights_one.reshape(span_second * span_third, rank))
    flat = lax.optimization_barrier(tensor.reshape(span_first, span_second * span_third))
    first_whole = jnp.dot(flat, weights_one, preferred_element_type=jnp.float32)
    first_whole = first_whole + jnp.dot(matrix, column_half, preferred_element_type=jnp.float32)
    rows_one = reduce_rows(first_whole, ("ja", "ka"), n_jk)
    partial_one = gather_rows(rows_one, ALL, n_all).reshape(span_first * n_ia, rank)
    raw_one = solve_rows(partial_one, inverse_factor(system_one))
    first_new = raw_one * column_scale(raw_one, span_first * n_ia)
    gram_first = gram_of(first_new)
    per_first = span_first // n_jk
    first_out = lax.dynamic_slice_in_dim(first_new, at * per_first, per_first, 0)
    first_half = lax.dynamic_slice_in_dim(first_new, at_ia * span_first, span_first, 0).astype(
        jnp.bfloat16
    )

    weights_two = (first_half.astype(jnp.float32)[:, None, :] * third_in[None, :, :]).astype(
        jnp.bfloat16
    )
    second_whole = lax.dot_general(
        tensor, weights_two, (((0, 2), (0, 1)), ((), ())), preferred_element_type=jnp.float32
    )
    n_ik = n_ia * n_ka
    per_second = span_second // n_ik
    rows_two = reduce_rows(second_whole, ("ia", "ka"), n_ik)
    partial_two = gather_rows(rows_two, ALL, n_all).reshape(n_all * per_second, rank)
    raw_two = solve_rows(partial_two, inverse_factor(gram_first * gram_third))
    second_new = raw_two * column_scale(raw_two, span_second * n_ja)
    gram_updated = gram_of(second_new)
    second_out = lax.dynamic_slice_in_dim(second_new, at * per_second, per_second, 0)
    blocks = second_new.reshape(n_ia, n_ja, n_ka, per_second, rank)
    second_half = (
        lax.dynamic_index_in_dim(blocks, at_ja, 1, keepdims=False)
        .reshape(span_second, rank)
        .astype(jnp.bfloat16)
    )

    weights_three = (first_half[:, None, :] * second_half[None, :, :]).reshape(
        span_first * span_second, rank
    )
    third_whole = lax.dot_general(
        tensor.reshape(span_first * span_second, span_third),
        weights_three,
        (((0,), (0,)), ((), ())),
        preferred_element_type=jnp.float32,
    )
    column_whole = lax.dot_general(
        matrix, first_half, (((0,), (0,)), ((), ())), preferred_element_type=jnp.float32
    )
    rows_column = reduce_rows(column_whole, "ia", n_ia)
    raw_column = solve_rows(rows_column, inverse_factor(gram_first))
    squares = jnp.sum(raw_column * raw_column, axis=0, keepdims=True)
    n_ij = n_ia * n_ja
    per_third = span_third // n_ij
    rows_three = reduce_rows(third_whole, ("ia", "ja"), n_ij)
    last = gather_rows(jnp.concatenate([rows_three, squares], axis=0), ALL, n_all)
    partial_three = last[:, :per_third].reshape(n_all * per_third, rank)
    raw_three = solve_rows(partial_three, inverse_factor(gram_first * gram_updated))
    third_new = raw_three * column_scale(raw_three, span_third * n_ka)
    third_out = lax.dynamic_slice_in_dim(third_new, at * per_third, per_third, 0)
    column_squares = jnp.sum(last[:, per_third], axis=0)
    column_out = raw_column * lax.rsqrt(column_squares / (span_column * n_jk) + 1e-06)
    return (first_out, second_out[None], third_out[None], column_out[None])


def solution(mesh):
    placed = (
        P("ia", "ja", "ka"),
        P("ia", ("ja", "ka")),
        P("ja", None),
        P("ka", None),
        P(("ja", "ka"), None),
    )
    return jax.shard_map(
        body,
        mesh=mesh,
        in_specs=placed,
        out_specs=(
            P(("ia", "ja", "ka"), None),
            P("ja", ("ia", "ka"), None),
            P("ka", ("ia", "ja"), None),
            P(("ja", "ka"), "ia", None),
        ),
        check_vma=False,
    )
```

```python
import jax
import jax.numpy as jnp
from jax import lax
from jax.experimental import pallas as pl
from jax.experimental.pallas import tpu as pltpu
from jax.sharding import PartitionSpec as P

ALL = ("ia", "ja", "ka")
HI = lax.Precision.HIGHEST
STEP = 32
GROUP = 8


def dot_on(left, right, left_dim, right_dim):
    return lax.dot_general(
        left,
        right,
        (((left_dim,), (right_dim,)), ((), ())),
        precision=HI,
        preferred_element_type=jnp.float32,
    )


def gram_of(factor):
    return dot_on(factor, factor, 0, 0)


def matmul(left, right):
    return dot_on(left, right, 1, 0)


def block_factor(block):
    size = block.shape[0]
    row = lax.broadcasted_iota(jnp.int32, (size, size), 0)
    col = lax.broadcasted_iota(jnp.int32, (size, size), 1)
    for first in range(0, size, GROUP):
        planes = [
            jnp.broadcast_to(block[:, first + m : first + m + 1], (size, size))
            for m in range(GROUP)
        ]
        for m in range(GROUP):
            k = first + m
            scale = lax.rsqrt(planes[m][k : k + 1, :])
            factor = jnp.where(row > k, planes[m] * scale, 0.0)
            for n in range(m + 1, GROUP):
                planes[n] = planes[n] - factor * (planes[n][k : k + 1, :] * scale)
            pivot = jnp.where(col[k : k + 1] == k, 1.0, block[k : k + 1, :]) * scale
            rest = jnp.where((col == k) & (row > k), 0.0, block)
            block = jnp.where(row == k, pivot, rest - factor * pivot)
    return jnp.where(col <= row, block, 0.0)


def inverse_kernel(*refs):
    count = len(refs) // 3
    systems, inverses, works = refs[:count], refs[count : 2 * count], refs[2 * count :]
    rank = systems[0].shape[0]
    for system, work in zip(systems, works):
        work[...] = system[...]
    for low in range(0, rank, STEP):
        high = low + STEP
        factors = [block_factor(work[low:high, low:high]) for work in works]
        for work, factor in zip(works, factors):
            if high < rank:
                below = work[high:, low:high]
            work[low:high, low:high] = jnp.eye(STEP, dtype=jnp.float32)
            rows = matmul(factor, work[low:high, :])
            if high < rank:
                work[high:, low:high] = jnp.zeros((rank - high, STEP), jnp.float32)
                work[high:, :] = work[high:, :] - matmul(dot_on(below, factor, 1, 1), rows)
            cols = lax.broadcasted_iota(jnp.int32, (STEP, rank), 1)
            work[low:high, :] = jnp.where(cols < high, rows, 0.0)
    for work, inverse in zip(works, inverses):
        factor = work[...]
        inverse[...] = dot_on(factor, factor, 0, 0)


def inverses_of(*systems):
    count = len(systems)
    rank = systems[0].shape[0]
    vmem = pl.BlockSpec(memory_space=pltpu.VMEM)
    return pl.pallas_call(
        inverse_kernel,
        out_shape=[jax.ShapeDtypeStruct((rank, rank), jnp.float32)] * count,
        in_specs=[vmem] * count,
        out_specs=[vmem] * count,
        scratch_shapes=[pltpu.VMEM((rank, rank), jnp.float32)] * count,
        cost_estimate=pl.CostEstimate(
            flops=2000000000 * count, transcendentals=0, bytes_accessed=30000000 * count
        ),
        compiler_params=pltpu.CompilerParams(vmem_limit_bytes=16 << 20),
    )(*systems)


def exchange(blocks, axes):
    return lax.all_to_all(blocks, axes, 0, 0, tiled=True)


def reduce_rows(whole, axes, parts):
    rows, width = whole.shape
    return jnp.sum(exchange(whole.reshape(parts, rows // parts, width), axes), axis=0)


def gather_rows(rows, axes, parts):
    return exchange(jnp.broadcast_to(rows[None], (parts,) + rows.shape), axes)


def column_scale(unscaled, row_total):
    return lax.rsqrt(jnp.sum(unscaled * unscaled, axis=0) / row_total + 1e-06)


def body(tensor, matrix, second_in, third_in, column_in):
    span_first, span_second, span_third = tensor.shape
    span_column = matrix.shape[1]
    rank = second_in.shape[1]
    n_ia, n_ja, n_ka = (lax.axis_size(a) for a in ALL)
    n_all = n_ia * n_ja * n_ka
    n_jk = n_ja * n_ka
    at_ia, at_ja, at_ka = (lax.axis_index(a) for a in ALL)
    at = (at_ia * n_ja + at_ja) * n_ka + at_ka

    other = lax.ppermute(third_in, "ka", [(0, 1), (1, 0)])
    part_second = span_second // n_ka
    half = rank // 2
    slab = half // n_ia
    gram_second = gram_of(lax.dynamic_slice_in_dim(second_in, at_ka * part_second, part_second, 0))
    gram_column = gram_of(column_in)

    def slabs(gram):
        low = lax.dynamic_slice_in_dim(gram, at_ia * slab, slab, 0)
        high = lax.dynamic_slice_in_dim(gram, half + at_ia * slab, slab, 0)
        return jnp.stack([low, high], axis=1)

    column_half = column_in.astype(jnp.bfloat16)
    weights_one = (second_in[:, None, :] * third_in[None, :, :]).astype(jnp.bfloat16)
    weights_one = lax.optimization_barrier(weights_one.reshape(span_second * span_third, rank))
    flat = lax.optimization_barrier(tensor.reshape(span_first, span_second * span_third))
    first_whole = jnp.dot(flat, weights_one, preferred_element_type=jnp.float32)
    first_whole = first_whole + jnp.dot(matrix, column_half, preferred_element_type=jnp.float32)
    per_first = span_first // n_jk
    sent = jnp.concatenate(
        [first_whole.reshape(n_jk, per_first, rank), slabs(gram_second), slabs(gram_column)],
        axis=1,
    )
    sums = jnp.sum(exchange(sent, ("ja", "ka")), axis=0)
    gram_third = gram_of(third_in) + gram_of(other)
    rows_third = jnp.concatenate(
        [
            lax.dynamic_slice_in_dim(gram_third, at_ia * n_jk + at_ja * n_ka + at_ka, 1, 0),
            lax.dynamic_slice_in_dim(gram_third, half + at_ia * n_jk + at_ja * n_ka + at_ka, 1, 0),
        ],
        axis=0,
    )
    rows_system = sums[per_first : per_first + 2] * rows_third + sums[per_first + 2 :]
    gathered = gather_rows(jnp.concatenate([sums[:per_first], rows_system], axis=0), ALL, n_all)
    partial_one = gathered[:, :per_first].reshape(span_first * n_ia, rank)
    system_one = jnp.concatenate([gathered[:, per_first], gathered[:, per_first + 1]], axis=0)
    (inverse_one,) = inverses_of(system_one)
    raw_one = matmul(partial_one, inverse_one)
    first_new = raw_one * column_scale(raw_one, span_first * n_ia)
    gram_first = gram_of(first_new)
    first_out = lax.dynamic_slice_in_dim(first_new, at * per_first, per_first, 0)
    first_half = lax.dynamic_slice_in_dim(first_new, at_ia * span_first, span_first, 0).astype(
        jnp.bfloat16
    )

    weights_two = (first_half.astype(jnp.float32)[:, None, :] * third_in[None, :, :]).astype(
        jnp.bfloat16
    )
    second_whole = lax.dot_general(
        tensor, weights_two, (((0, 2), (0, 1)), ((), ())), preferred_element_type=jnp.float32
    )
    n_ik = n_ia * n_ka
    per_second = span_second // n_ik
    rows_two = reduce_rows(second_whole, ("ia", "ka"), n_ik)
    partial_two = gather_rows(rows_two, ALL, n_all).reshape(n_all * per_second, rank)
    inverse_two, inverse_column = inverses_of(gram_first * gram_third, gram_first)
    raw_two = matmul(partial_two, inverse_two)
    second_new = raw_two * column_scale(raw_two, span_second * n_ja)
    gram_updated = gram_of(second_new)
    second_out = lax.dynamic_slice_in_dim(second_new, at * per_second, per_second, 0)
    blocks = second_new.reshape(n_ia, n_ja, n_ka, per_second, rank)
    second_half = (
        lax.dynamic_index_in_dim(blocks, at_ja, 1, keepdims=False)
        .reshape(span_second, rank)
        .astype(jnp.bfloat16)
    )

    weights_three = (first_half[:, None, :] * second_half[None, :, :]).reshape(
        span_first * span_second, rank
    )
    third_whole = lax.dot_general(
        tensor.reshape(span_first * span_second, span_third),
        weights_three,
        (((0,), (0,)), ((), ())),
        preferred_element_type=jnp.float32,
    )
    column_whole = lax.dot_general(
        matrix, first_half, (((0,), (0,)), ((), ())), preferred_element_type=jnp.float32
    )
    rows_column = reduce_rows(column_whole, "ia", n_ia)
    raw_column = matmul(rows_column, inverse_column)
    squares = jnp.sum(raw_column * raw_column, axis=0, keepdims=True)
    n_ij = n_ia * n_ja
    per_third = span_third // n_ij
    rows_three = reduce_rows(third_whole, ("ia", "ja"), n_ij)
    last = gather_rows(jnp.concatenate([rows_three, squares], axis=0), ALL, n_all)
    partial_three = last[:, :per_third].reshape(n_all * per_third, rank)
    (inverse_three,) = inverses_of(gram_first * gram_updated)
    raw_three = matmul(partial_three, inverse_three)
    third_new = raw_three * column_scale(raw_three, span_third * n_ka)
    third_out = lax.dynamic_slice_in_dim(third_new, at * per_third, per_third, 0)
    column_squares = jnp.sum(last[:, per_third], axis=0)
    column_out = raw_column * lax.rsqrt(column_squares / (span_column * n_jk) + 1e-06)
    return (first_out, second_out[None], third_out[None], column_out[None])


def solution(mesh):
    placed = (
        P("ia", "ja", "ka"),
        P("ia", ("ja", "ka")),
        P("ja", None),
        P("ka", None),
        P(("ja", "ka"), None),
    )
    return jax.shard_map(
        body,
        mesh=mesh,
        in_specs=placed,
        out_specs=(
            P(("ia", "ja", "ka"), None),
            P("ja", ("ia", "ka"), None),
            P("ka", ("ia", "ja"), None),
            P(("ja", "ka"), "ia", None),
        ),
        check_vma=False,
    )
```
